32 devices in a mesh: section: 2 (over core), dp: 16 (over z, y, x).
Axes of the slice: x: 2, y: 2, z: 4, core: 2. Of those that a mesh axis runs over, the one named last changes fastest.
Arguments:
- states: bfloat16 [2, 6144, 4096], P('section', 'dp'), may hold values from -6 to 6
- mix_logits: float32 [2], replicated, may hold values from -3 to 303
- mix_gamma: float32 [1], replicated, may hold values from 0.5 to 2
- tag_w1: bfloat16 [4096, 3072], P(None, 'section'), may hold values from -0.09375 to 0.09375
- tag_b1: float32 [3072], P('section'), may hold values from -3 to 3
- tag_w2: bfloat16 [3072, 4], P('section'), may hold values from -0.3125 to 0.3125
- tag_b2: float32 [4], replicated, may hold values from -3 to 3
- hyp_lengths: int32 [16], P('dp'), may hold values from 48 to 192, as said below
- labels: int32 [6144], P('dp'), may hold values from 0 to 3
Outputs:
- loss: float32 [1], replicated
- grad_w1: float32 [4096, 3072], P('dp', 'section')
- grad_b1: float32 [3072], P('section')
- grad_w2: float32 [3072, 4], P('section')
- grad_b2: float32 [4], replicated
- grad_mix: float32 [2], replicated
- grad_gamma: float32 [1], replicated
- grad_states: bfloat16 [2, 6144, 4096], P('section', 'dp')
The draws below stay inside these ranges and needn't reach their ends.
Inputs may be any that keep to these rules, and one draw needn't show every extreme that they name: `hyp_lengths`: triplet r's hypothesis covers positions 1 to hyp_lengths_r of its 384 tokens.
All inputs are finite; a program needn't handle non-finite values.
Results may differ from the reference program's by a relative error of at most 0.03.
Values may be sent and summed in bfloat16 or wider, within the bound.
No kernel may reach another device: no remote copies, remote signals or barrier semaphores. Data moves between devices by JAX's collectives and lax.ppermute only.
A program may use at most 128 MiB of HBM per device.

```python
import math
import jax
import jax.numpy as jnp
from jax import lax

D = 4096
FF_TAG = 3072
CLASSES = 4
LAYERS_DEV = 1
TOK_DEV = 384
STATES = 2
TOKENS = 6144
N_SECTION = 2
N_DP = 16


def draw_mix_logits(key, part):
    values = jax.random.uniform(key, (STATES,), jnp.float32, -3.0, 3.0)
    return values


def draw_hyp_lengths(key, part):
    low = TOK_DEV // 8
    high = TOK_DEV // 2
    order_key = jax.random.fold_in(key, 11)
    jitter_key = jax.random.fold_in(key, 23)
    ranks = jax.random.permutation(order_key, N_DP).astype(jnp.int32)
    base = low + (high - low) * ranks // max(N_DP - 1, 1)
    jitter = jax.random.randint(jitter_key, (N_DP,), 0, max((high - low) // 4, 2))
    values = jnp.minimum(base + jitter, high)
    values = jnp.where(ranks == 0, low, values)
    values = jnp.where(ranks == N_DP - 1, high, values)
    return values.astype(jnp.int32)


def touch_ends(values, key, low, largest):
    shape = values.shape
    place = [jax.random.randint(jax.random.fold_in(key, axis), (), 0, shape[axis]) for axis in range(len(shape))]
    values = values.at[tuple(place)].set(low)
    longest = shape.index(max(shape))
    place[longest] = (place[longest] + 1) % shape[longest]
    return values.at[tuple(place)].set(largest)


def shard_levels(own_key, dims, pieces, low, high):
    def one(position, blocks):
        draws = jax.random.uniform(jax.random.fold_in(jax.random.fold_in(own_key, 6), position), (blocks,), jnp.float32, low / len(pieces), high / len(pieces))
        return jnp.repeat(jnp.exp(draws), dims[position] // blocks).reshape((-1,) + (1,) * (len(dims) - position - 1))

    level = one(*pieces[0])
    for cut in pieces[1:]:
        level = level * one(*cut)
    return level


def scatter_about(stream_key, shape, scale, bound, cuts=(), held_as=jnp.bfloat16):
    loudness = shard_levels(stream_key, shape, cuts, -0.22, 0.18) if cuts else 1.0
    values = jax.random.normal(stream_key, shape, jnp.float32) * scale * loudness
    return jnp.minimum(jnp.maximum(values, -bound), bound).astype(held_as)


def setup_inputs(seed: int = 0) -> dict:
    arg_keys = jax.random.split(jax.random.key(seed), 10)
    states = scatter_about(arg_keys[0], (STATES, TOKENS, D), 1.0, 6.0, ((0, 2), (1, 16)))
    mix_logits = draw_mix_logits(jax.random.fold_in(arg_keys[9], 71), 0)
    mix_gamma = jnp.clip(jnp.exp(jax.random.uniform(arg_keys[2], (1,), jnp.float32, math.log(0.5), math.log(2.0))), 0.5, 2.0)
    tag_w1 = scatter_about(arg_keys[3], (D, FF_TAG), D ** -0.5, 0.09375, ((1, 2),))
    tag_b1 = scatter_about(arg_keys[4], (FF_TAG,), 0.5, 3.0, ((0, 2),), jnp.float32)
    tag_w2 = scatter_about(arg_keys[5], (FF_TAG, CLASSES), (FF_TAG // 8) ** -0.5, 0.3125, ((0, 2),))
    tag_b2 = scatter_about(arg_keys[6], (CLASSES,), 1.0, 3.0, (), jnp.float32)
    hyp_lengths = draw_hyp_lengths(jax.random.fold_in(arg_keys[9], 71), 0)
    labels = touch_ends(jax.random.randint(arg_keys[8], (TOKENS,), 0, CLASSES), jax.random.fold_in(arg_keys[8], 1), 0, CLASSES - 1).astype(jnp.int32)
    return {"states": states, "mix_logits": mix_logits, "mix_gamma": mix_gamma, "tag_w1": tag_w1, "tag_b1": tag_b1, "tag_w2": tag_w2, "tag_b2": tag_b2, "hyp_lengths": hyp_lengths, "labels": labels}


def gelu_parts(pre):
    cdf = 0.5 * (1.0 + lax.erf(pre * 0.7071067811865476))
    dens = jnp.exp(-0.5 * pre * pre) * 0.3989422804014327
    return pre * cdf, cdf + pre * dens


def reference(states, mix_logits, mix_gamma, tag_w1, tag_b1, tag_w2, tag_b2, hyp_lengths, labels):
    top = jnp.max(mix_logits)
    expo = jnp.exp(mix_logits - top)
    weights = expo / jnp.sum(expo)
    gamma = mix_gamma[0]
    positions = jnp.arange(TOK_DEV, dtype=jnp.int32)
    masks = ((positions[None, :] >= 1) & (positions[None, :] <= hyp_lengths[:, None])).astype(jnp.float32)
    count = jnp.sum(masks)
    section_w = weights.reshape(N_SECTION, LAYERS_DEV)
    group = FF_TAG // N_SECTION
    w1_split = tag_w1.astype(jnp.float32).reshape(D, N_SECTION, group)
    classes = jnp.arange(CLASSES, dtype=jnp.int32)

    def per_replica(carry, index):
        gw1, gb1, gw2, gb2, loss, scores = carry
        block = lax.dynamic_slice_in_dim(states, index * TOK_DEV, TOK_DEV, 1)
        block = block.reshape(N_SECTION, LAYERS_DEV, TOK_DEV, D)
        terms = jnp.sum(section_w[:, :, None, None] * block.astype(jnp.float32), axis=1).astype(jnp.bfloat16)
        terms = lax.optimization_barrier(terms)
        mixed = (gamma * jnp.sum(terms.astype(jnp.float32), axis=0)).astype(jnp.bfloat16)
        pre = jnp.dot(mixed, tag_w1, preferred_element_type=jnp.float32) + tag_b1
        act, slope = gelu_parts(pre)
        hidden = act.astype(jnp.bfloat16)
        logits = jnp.dot(hidden, tag_w2, preferred_element_type=jnp.float32) + tag_b2
        mask = lax.dynamic_index_in_dim(masks, index, 0, keepdims=False)
        lab = lax.dynamic_slice_in_dim(labels, index * TOK_DEV, TOK_DEV, 0)
        onehot = (lab[:, None] == classes[None, :]).astype(jnp.float32)
        expl = jnp.exp(logits)
        total = jnp.sum(expl, axis=1)
        ce = jnp.log(total) - jnp.sum(logits * onehot, axis=1)
        dlogits = mask[:, None] * (expl / total[:, None] - onehot) / count
        dlog16 = dlogits.astype(jnp.bfloat16)
        dhidden = jnp.dot(dlog16, tag_w2.T, preferred_element_type=jnp.float32)
        dpre = (dhidden * slope).astype(jnp.bfloat16)
        parts = jnp.einsum('tsf,dsf->std', dpre.astype(jnp.float32).reshape(TOK_DEV, N_SECTION, group), w1_split)
        parts = lax.optimization_barrier(parts.astype(jnp.bfloat16))
        dmixed = jnp.sum(parts.astype(jnp.float32), axis=0).astype(jnp.bfloat16)
        local_scores = jnp.einsum('sltd,td->sl', block.astype(jnp.float32), dmixed.astype(jnp.float32)).reshape(-1)
        dstates = (gamma * weights[:, None, None] * dmixed.astype(jnp.float32)[None]).astype(jnp.bfloat16)
        gw1 = gw1 + lax.dot_general(mixed, dpre, (((0,), (0,)), ((), ())), preferred_element_type=jnp.float32)
        gb1 = gb1 + jnp.sum(dpre.astype(jnp.float32), axis=0)
        gw2 = gw2 + jnp.dot(hidden.T, dlog16, preferred_element_type=jnp.float32)
        gb2 = gb2 + jnp.sum(dlogits, axis=0)
        loss = loss + jnp.sum(mask * ce) / count
        scores = scores + local_scores
        return (gw1, gb1, gw2, gb2, loss, scores), dstates

    init = (jnp.zeros((D, FF_TAG), jnp.float32), jnp.zeros((FF_TAG,), jnp.float32),
            jnp.zeros((FF_TAG, CLASSES), jnp.float32), jnp.zeros((CLASSES,), jnp.float32),
            jnp.zeros((), jnp.float32), jnp.zeros((STATES,), jnp.float32))
    carry, dstates = lax.scan(per_replica, init, jnp.arange(N_DP, dtype=jnp.int32))
    gw1, gb1, gw2, gb2, loss, scores = carry
    grad_gamma = jnp.sum(weights * scores)
    grad_mix = gamma * weights * (scores - grad_gamma)
    grad_states = jnp.transpose(dstates, (1, 0, 2, 3)).reshape(STATES, TOKENS, D)
    return (loss.reshape(1), gw1, gb1, gw2, gb2, grad_mix, grad_gamma.reshape(1), grad_states)
```

```python
import jax
import jax.numpy as jnp
from jax import lax
from jax.sharding import PartitionSpec as P

CHUNKS = 2


def gelu_parts(pre):
    cdf = 0.5 * (1.0 + lax.erf(pre * 0.7071067811865476))
    dens = jnp.exp(-0.5 * pre * pre) * 0.3989422804014327
    return (pre * cdf, cdf + pre * dens)


def flip(x, axis, size, bit):
    return lax.ppermute(x, axis, [(i, i ^ bit) for i in range(size)])


def others(x, axis, size):
    return [flip(x, axis, size, k) for k in range(1, size)]


def split_dp(n_dp):
    inner = 1
    while inner * inner < n_dp:
        inner *= 2
    return n_dp // inner, inner


def gather_outer(x, n_outer, n_inner):
    n_dp = n_outer * n_inner
    if n_outer != 4:
        return [flip(x, "dp", n_dp, k * n_inner) for k in range(1, n_outer)]
    pairs = lambda links: [(a * n_inner + i, b * n_inner + i) for a, b in links for i in range(n_inner)]
    one = flip(x, "dp", n_dp, n_inner)
    two = flip(x, "dp", n_dp, 2 * n_inner)
    middle = lax.ppermute(x, "dp", pairs([(1, 2), (2, 1)]))
    ends = lax.ppermute(two, "dp", pairs([(1, 0), (2, 3)]))
    return [one, two, middle + ends]


def scatter_inner(blocks, inner_idx, n_outer, n_inner, order):
    n_dp = n_outer * n_inner
    own = blocks
    left = list(range(n_inner))
    for bit in order:
        send = [j for j in left if j & bit]
        left = [j for j in left if not j & bit]
        got = flip(jnp.concatenate([own[j] for j in send], 0), "dp", n_dp, bit)
        rows = got.shape[0] // len(send)
        own = dict(
            (j, (own[j].astype(jnp.float32) + got[i * rows : (i + 1) * rows].astype(jnp.float32)).astype(jnp.bfloat16))
            for i, j in enumerate(left)
        ) if bit != order[-1] else dict(
            (j, own[j].astype(jnp.float32) + got[i * rows : (i + 1) * rows].astype(jnp.float32)) for i, j in enumerate(left)
        )
    return own[0]


def make_shards(n_section, n_dp):
    n_outer, n_inner = split_dp(n_dp)
    bits = [1 << b for b in range(n_inner.bit_length() - 1)]

    def shards(states, mix_logits, mix_gamma, tag_w1, tag_b1, tag_w2, tag_b2, hyp_lengths, labels):
        layers, tok, width = states.shape
        ff = tag_w1.shape[1]
        classes = tag_b2.shape[0]
        f32, bf16 = jnp.float32, jnp.bfloat16
        half = tok // 2
        section_idx = lax.axis_index("section")
        dp_idx = lax.axis_index("dp")
        outer_idx, inner_idx = dp_idx // n_inner, dp_idx % n_inner

        def window(x):
            row = lax.broadcasted_iota(jnp.int32, (half,) + (1,) * (x.ndim - 1), 0)
            return jnp.where(row == 0, x[half : half + 1], x[:half])

        top = jnp.max(mix_logits)
        expo = jnp.exp(mix_logits - top)
        weights = expo / jnp.sum(expo)
        local_w = lax.dynamic_slice_in_dim(weights, section_idx * layers, layers)
        gamma = mix_gamma[0]

        term = sum(local_w[l] * window(states[l]).astype(f32) for l in range(layers)).astype(bf16)
        total = term.astype(f32)
        for part in others(term, "section", n_section):
            total = total + part.astype(f32)
        mixed = (gamma * total).astype(bf16)

        share = half // n_section
        out_cols = width // n_outer
        mine = lax.dynamic_slice_in_dim(mixed, section_idx * share, share, 0)
        lefts = [lax.dynamic_slice_in_dim(mixed, outer_idx * out_cols, out_cols, 1)]
        for k in range(1, n_outer):
            cols = lax.dynamic_slice_in_dim(mine, (outer_idx ^ k) * out_cols, out_cols, 1)
            got = flip(cols, "dp", n_dp, k * n_inner)
            parts = [got] + others(got, "section", n_section)
            full = jnp.zeros((n_section, share, out_cols), bf16)
            for j, part in enumerate(parts):
                full = lax.dynamic_update_slice_in_dim(full, part[None], section_idx ^ j, 0)
            lefts.append(full.reshape(half, out_cols))

        pre = jnp.dot(mixed, tag_w1, preferred_element_type=f32) + tag_b1
        act, slope = gelu_parts(pre)
        hidden = act.astype(bf16)
        partial = lax.dot_general(tag_w2, hidden, (((0,), (1,)), ((), ())), preferred_element_type=f32)
        logits = partial
        for part in others(partial, "section", n_section):
            logits = logits + part
        logits = logits + tag_b2[:, None]

        lab = window(labels)
        position = jnp.arange(half, dtype=jnp.int32)
        mask = (jnp.where(position == 0, half, position) <= hyp_lengths[0]).astype(f32)
        onehot = (lab[None, :] == jnp.arange(classes, dtype=jnp.int32)[:, None]).astype(f32)
        expl = jnp.exp(logits)
        totals = jnp.sum(expl, axis=0)
        entropy = jnp.log(totals) - jnp.sum(logits * onehot, axis=0)
        dlogits = mask * (expl / totals - onehot)
        dlog16 = dlogits.astype(bf16)
        dhidden = lax.dot_general(dlog16, tag_w2, (((0,), (1,)), ((), ())), preferred_element_type=f32)
        dpre = (dhidden * slope).astype(bf16)

        step = ff // CHUNKS
        lhs = jnp.concatenate(lefts, 0)
        lhs = lhs.reshape(n_outer * half, n_inner, out_cols // n_inner)
        chunks = []
        for c in range(CHUNKS):
            piece = dpre[:, c * step : (c + 1) * step]
            rhs = jnp.concatenate([piece] + gather_outer(piece, n_outer, n_inner), 0)
            halves = []
            for h, order in enumerate((bits, bits[::-1])):
                cut = rhs[:, h * (step // 2) : (h + 1) * (step // 2)]
                blocks = {}
                for j in range(n_inner):
                    a = lax.dynamic_index_in_dim(lhs, inner_idx ^ j, 1, keepdims=False)
                    blocks[j] = lax.dot_general(a, cut, (((0,), (0,)), ((), ())), preferred_element_type=f32).astype(bf16)
                halves.append(scatter_inner(blocks, inner_idx, n_outer, n_inner, order))
            chunks += halves

        part = lax.dot_general(dpre, tag_w1, (((1,), (1,)), ((), ())), preferred_element_type=f32).astype(bf16)
        dmixed = part.astype(f32)
        for other in others(part, "section", n_section):
            dmixed = dmixed + other.astype(f32)
        dmixed = dmixed.astype(bf16)
        scores = jnp.stack([jnp.sum(window(states[l]).astype(f32) * dmixed.astype(f32)) for l in range(layers)])

        local_w2 = lax.dot_general(dlog16, hidden, (((1,), (0,)), ((), ())), preferred_element_type=f32)
        local_b1 = jnp.sum(dpre.astype(f32), axis=0, keepdims=True)
        misc = jnp.concatenate(
            [jnp.sum(dlogits, axis=1), jnp.sum(mask * entropy)[None], jnp.sum(mask)[None], scores]
        )
        misc = jnp.pad(misc, (0, ff - misc.shape[0]))[None]
        small = jnp.concatenate([local_w2, local_b1, misc], 0)
        bit = 1
        while bit < n_dp:
            small = small + flip(small, "dp", n_dp, bit)
            bit *= 2
        inv = 1.0 / small[classes + 1, classes + 1]
        small = small * inv
        misc = small[classes + 1]
        local_scores = misc[classes + 2 : classes + 2 + layers]
        gathered = jnp.zeros((n_section, layers), f32)
        for j, other in enumerate([local_scores] + others(local_scores, "section", n_section)):
            gathered = lax.dynamic_update_slice_in_dim(gathered, other[None], section_idx ^ j, 0)
        all_scores = gathered.reshape(-1)
        grad_gamma = jnp.sum(weights * all_scores)
        grad_mix = gamma * weights * (all_scores - grad_gamma)

        scaled = dmixed.astype(f32) * inv
        body = jnp.where(jnp.arange(half)[:, None] == 0, 0.0, scaled)
        rows = jnp.concatenate([body, scaled[:1], jnp.zeros((tok - half - 1, width), f32)], 0)
        grad_states = (gamma * local_w[:, None, None] * rows[None]).astype(bf16)
        grad_w1 = jnp.concatenate(chunks, 1) * inv
        return (
            misc[classes].reshape(1),
            grad_w1,
            small[classes],
            small[:classes].T,
            misc[:classes],
            grad_mix,
            grad_gamma.reshape(1),
            grad_states,
        )

    return shards


def solution(mesh):
    in_specs = (
        P("section", "dp", None),
        P(),
        P(),
        P(None, "section"),
        P("section"),
        P("section", None),
        P(),
        P("dp"),
        P("dp"),
    )
    out_specs = (
        P(),
        P("dp", "section"),
        P("section"),
        P("section", None),
        P(),
        P(),
        P(),
        P("section", "dp", None),
    )
    shards = make_shards(mesh.shape["section"], mesh.shape["dp"])
    return jax.shard_map(shards, mesh=mesh, in_specs=in_specs, out_specs=out_specs, check_vma=False)
```

```python
import functools

import jax
import jax.numpy as jnp
from jax import lax
from jax.experimental import pallas as pl
from jax.experimental.pallas import tpu as pltpu
from jax.sharding import PartitionSpec as P


CHUNKS = 4
COLS = 1024
F32, BF16 = jnp.float32, jnp.bfloat16
SDS = jax.ShapeDtypeStruct
SMEM = pl.BlockSpec(memory_space=pltpu.SMEM)
VMEM = pl.BlockSpec(memory_space=pltpu.VMEM)
ANY = pl.BlockSpec(memory_space=pl.ANY)


def call(body, grid, in_specs, out_specs, out_shape, scratch=(), limit=12, aliases={}):
    return pl.pallas_call(
        body,
        grid_spec=pltpu.PrefetchScalarGridSpec(
            num_scalar_prefetch=0, grid=grid, in_specs=in_specs, out_specs=out_specs, scratch_shapes=list(scratch)
        ),
        out_shape=out_shape,
        input_output_aliases=aliases,
        compiler_params=pltpu.CompilerParams(vmem_limit_bytes=limit << 20),
    )


def whole(shape):
    return pl.BlockSpec(tuple(shape), lambda *_: (0,) * len(shape))


def flip(x, axis, size, bit):
    return lax.ppermute(x, axis, [(i, i ^ bit) for i in range(size)])


def others(x, axis, size):
    return [flip(x, axis, size, k) for k in range(1, size)]


def chunk_widths(ff):
    tiles = ff // 128
    count = min(CHUNKS, tiles)
    return [128 * ((tiles + c) // count) for c in range(count)]


def split_dp(n_dp):
    bits = [1 << b for b in range(n_dp.bit_length() - 1)]
    gather = bits[0::2][: len(bits) // 2]
    return gather, [b for b in bits if b not in gather]


def spread(r, bits):
    out = 0
    for i, bit in enumerate(bits):
        out = out | (((r >> i) & 1) * bit)
    return out


def compress(dp, bits):
    out = 0
    for i, bit in enumerate(bits):
        out = out | (((dp // bit) & 1) << i)
    return out


def softmax_row(logits):
    lane = lax.broadcasted_iota(jnp.int32, (1, 128), 1)
    row = jnp.full((1, 128), -jnp.inf, F32)
    for s in range(logits.shape[0]):
        row = jnp.where(lane == s, logits[s], row)
    expo = jnp.exp(row - jnp.max(row, axis=1, keepdims=True))
    return expo / jnp.sum(expo, axis=1, keepdims=True)


def pick(row, index):
    lane = lax.broadcasted_iota(jnp.int32, row.shape, 1)
    return jnp.sum(jnp.where(lane == index, row, 0.0), axis=1, keepdims=True)


def first_rows(x, last):
    row = lax.broadcasted_iota(jnp.int32, last.shape, 0)
    return jnp.where(row == 0, last[:1].astype(F32), x[:16].astype(F32))


def split16(x):
    high = x.astype(BF16)
    return jnp.concatenate([high.astype(F32), x - high.astype(F32)], 0).astype(BF16)


def join16(x):
    x = x.astype(F32)
    n = x.shape[0] // 2
    return x[:n] + x[n:]


def term_body(layers, logits, x, last, w1, out, w1_part, sem):
    step, load = pl.program_id(0), pltpu.make_async_copy(w1.at[:, pl.ds(0, w1_part.shape[1])], w1_part, sem)

    @pl.when(step == 0)
    def _():
        load.start()

    weights = softmax_row(logits)
    section = lax.axis_index("section")
    scale = [pick(weights, section * layers + l) for l in range(layers)]
    head = sum(scale[l] * first_rows(x[l], last[l]) for l in range(layers))
    rest = sum(scale[l] * x[l, 16:].astype(F32) for l in range(layers))
    out[:16] = head.astype(BF16)
    out[16:] = rest.astype(BF16)

    @pl.when(step == pl.num_programs(0) - 1)
    def _():
        load.wait()


def load_body(first, w1, w1_part, sem):
    load = pltpu.make_async_copy(w1.at[:, pl.ds(first, w1_part.shape[1])], w1_part, sem)
    load.start()
    load.wait()


def mix_body(n, rows, blocks, gather, reduce, *refs):
    terms, gamma, mixed, sends = refs[:n], refs[n], refs[n + 1], refs[n + 2 :]
    total = terms[0][...].astype(F32)
    for t in terms[1:]:
        total = total + t[...].astype(F32)
    mixed[...] = (gamma[0] * total).astype(BF16)
    section, dp = lax.axis_index("section"), lax.axis_index("dp")
    own = dp - spread(compress(dp, reduce), reduce)
    for k, send in enumerate(sends, 1):
        for i in range(blocks):
            at = (own ^ spread(k, gather)) + spread(section * blocks + i, reduce)
            send[:, i * rows : (i + 1) * rows] = mixed[:, pl.ds(pl.multiple_of(at * rows, rows), rows)]


def pre_body(mixed, wa, wb, w1, b1, w2, hidden, slope, logits, wc, sem):
    step, wide = pl.program_id(0), hidden.shape[1]
    begin = wa.shape[1] + wb.shape[1]
    load = pltpu.make_async_copy(w1.at[:, pl.ds(begin, wc.shape[1])], wc, sem)

    @pl.when(step == 0)
    def _():
        load.start()
        logits[...] = jnp.zeros_like(logits)

    @pl.when(step == begin // wide)
    def _():
        load.wait()

    def side(w, first):
        cols = w[:, pl.ds(pl.multiple_of((step - first) * wide, wide), wide)]
        pre = jnp.dot(mixed[...], cols, preferred_element_type=F32) + b1[...]
        cdf = 0.5 * (1.0 + lax.erf(pre * 0.7071067811865476))
        dens = jnp.exp(-0.5 * pre * pre) * 0.3989422804014327
        act = (pre * cdf).astype(BF16)
        hidden[...] = act
        slope[...] = cdf + pre * dens
        logits[...] += lax.dot_general(w2[...], act, (((1,), (1,)), ((), ())), preferred_element_type=F32)

    first = 0
    for w in (wa, wb, wc):
        count = w.shape[1] // wide
        pl.when((step >= first) & (step < first + count))(functools.partial(side, w, first))
        first += count


def loss_body(n, widths, extra, *refs):
    chunks = len(widths)
    parts = refs[:n]
    b2, labels, hyp, w2, hidden, slope = refs[n : n + 6]
    dpre, pieces = refs[n + 6], refs[n + 7 : n + 7 + chunks]
    logits = parts[0][...]
    for p in parts[1:]:
        logits = logits + p[...]
    classes, half = logits.shape
    kind = lax.broadcasted_iota(jnp.int32, logits.shape, 0)
    for c in range(classes):
        logits = logits + jnp.where(kind == c, b2[c], 0.0)
    lane = lax.broadcasted_iota(jnp.int32, (1, half), 1)
    mask = (jnp.where(lane == 0, half, lane) <= hyp[0]).astype(F32)
    lab = labels[...]
    lab = jnp.where(lane == 0, lab[:, half : half + 1], lab[:, :half])
    onehot = (kind == lab).astype(F32)
    expl = jnp.exp(logits)
    totals = jnp.sum(expl, axis=0, keepdims=True)
    entropy = jnp.log(totals) - jnp.sum(logits * onehot, axis=0, keepdims=True)
    dlogits = mask * (expl / totals - onehot)
    dlog16 = dlogits.astype(BF16)
    dhidden = lax.dot_general(dlog16, w2[...], (((0,), (0,)), ((), ())), preferred_element_type=F32)
    grad = (dhidden * slope[...]).astype(BF16)
    dpre[...] = grad
    ff = grad.shape[1]
    grad_w2 = lax.dot_general(dlog16, hidden[...], (((1,), (0,)), ((), ())), preferred_element_type=F32)
    grad_b1 = jnp.sum(grad.astype(F32), axis=0, keepdims=True)
    col = lax.broadcasted_iota(jnp.int32, (1, ff), 1)
    row = jnp.where(col == classes, jnp.sum(mask * entropy), 0.0)
    row = jnp.where(col == classes + 1, jnp.sum(mask), row)
    sums = jnp.sum(dlogits, axis=1, keepdims=True)
    for c in range(classes):
        row = jnp.where(col == c, sums[c : c + 1], row)
    rows = [grad_w2, grad_b1, row]
    if extra // 2 > classes + 2:
        rows.append(jnp.zeros((extra // 2 - classes - 2, ff), F32))
    small = split16(jnp.concatenate(rows, 0))
    start = 0
    for piece, step in zip(pieces, widths):
        piece[0:half] = grad[:, start : start + step]
        piece[half:] = small[:, start : start + step]
        start += step


def dmixed_body(base, dpre, wa, wb, wc, out):
    tall = out.shape[1]
    row = pl.multiple_of((pl.program_id(0) + base) * tall, tall)
    total, col = None, 0
    for w in (wa, wb, wc):
        n = w.shape[1]
        part = lax.dot_general(
            dpre[:, col : col + n], w[pl.ds(row, tall)], (((1,), (1,)), ((), ())), preferred_element_type=F32
        )
        total = part if total is None else total + part
        col += n
    out[...] = total.astype(BF16)


def score_body(n, layers, *refs):
    parts, x, last, dmixed, scores = refs[: 2 * n], refs[2 * n], refs[2 * n + 1], refs[2 * n + 2], refs[2 * n + 3]
    step, steps = pl.program_id(0), pl.num_programs(0)

    @pl.when(step == 0)
    def _():
        scores[...] = jnp.zeros_like(scores)

    cols = x.shape[2]

    def side(some, first):
        at = pl.ds(pl.multiple_of((step - first) * cols, cols), cols)
        total = some[0][:, at].astype(F32)
        for p in some[1:]:
            total = total + p[:, at].astype(F32)
        d16 = total.astype(BF16)
        dmixed[:, pl.ds(pl.multiple_of(step * cols, cols), cols)] = d16
        d = d16.astype(F32)
        lane = lax.broadcasted_iota(jnp.int32, (1, 128), 1)
        section = lax.axis_index("section")
        for l in range(layers):
            prod = jnp.sum(first_rows(x[l], last[l]) * d[:16], axis=0, keepdims=True)
            prod = prod + jnp.sum(x[l, 16:].astype(F32) * d[16:], axis=0, keepdims=True)
            score = jnp.sum(prod, axis=1, keepdims=True)
            scores[0:1] += jnp.where(lane == section * layers + l, score, 0.0)

    @pl.when(step < steps // 2)
    def _():
        side(parts[:n], 0)

    @pl.when(step >= steps // 2)
    def _():
        side(parts[n:], steps // 2)


def total_body(*refs):
    total = refs[0][...]
    for s in refs[1:-1]:
        total = total + s[...]
    refs[-1][...] = total


def left_body(n, rows, blocks, reduce, *refs):
    mixed, gots, out = refs[0], refs[1:-1], refs[-1]
    section, dp = lax.axis_index("section"), lax.axis_index("dp")
    own = dp - spread(compress(dp, reduce), reduce)
    share = rows * blocks
    for j in range(n):
        cols = []
        for i in range(blocks):
            at = own + spread((section ^ j) * blocks + i, reduce)
            cols.append(mixed[:, pl.ds(pl.multiple_of(at * rows, rows), rows)])
        parts = [jnp.concatenate(cols, 1)] + [got[...] for got in gots[j::n]]
        out[pl.ds(pl.multiple_of((section ^ j) * share, share), share)] = jnp.concatenate(parts, 0).T


def halves(blocks, tail, send, keep, block_of, rows):
    for out, parity in ((send, 1), (keep, 0)):
        for i in range(blocks // 2):
            out[i * rows : (i + 1) * rows] = block_of(2 * i + parity)
    send[blocks // 2 * rows :] = tail


def weight_body(n_gather, half, reduce, *refs):
    left, pieces, (send, keep, small, rhs, prod) = refs[0], refs[1 : 1 + n_gather], refs[1 + n_gather :]
    r = compress(lax.axis_index("dp"), reduce)
    total = None
    for k, piece in enumerate(pieces):
        rhs[k * half : (k + 1) * half] = piece[:half]
        own = join16(piece[half:])
        total = own if total is None else total + own
    prod[...] = jnp.dot(left[...], rhs[...], preferred_element_type=F32).astype(BF16)
    small[...] = total
    blocks = 1 << len(reduce)
    rows = prod.shape[0] // blocks
    halves(
        blocks, split16(total), send, keep,
        lambda j: prod[pl.ds(pl.multiple_of((r ^ j) * rows, rows), rows)], rows,
    )


def add_body(rows, kept, got, small_in, send, keep, small):
    base = kept.shape[0]
    total = small_in[...] + join16(got[base:])
    small[...] = total
    block = lambda j: (
        kept[j * rows : (j + 1) * rows].astype(F32) + got[j * rows : (j + 1) * rows].astype(F32)
    ).astype(BF16)
    halves(base // rows, split16(total), send, keep, block, rows)


def final_body(chunk, chunks, classes, kept, got, small, *refs):
    if chunk:
        first, refs = refs[0], refs[2:]
    last = chunk == chunks - 1 and chunk > 0
    if last:
        mids, refs = refs[: chunks - 2], refs[chunks - 2 :]
    grad, total = refs[0], refs[1]
    strip = grad.shape[0]

    @pl.when(pl.program_id(0) == 0)
    def _():
        total[...] = small[...] + join16(got[kept.shape[0] :])

    misc = (first if chunk else total)[classes + 1 : classes + 2]
    inv = 1.0 / pick(misc, classes + 1)
    start = pl.multiple_of(pl.program_id(0) * strip, strip)
    grad[...] = (kept[pl.ds(start, strip)].astype(F32) + got[pl.ds(start, strip)].astype(F32)) * inv
    if last:
        gb1, gw2 = refs[2:]

        @pl.when(pl.program_id(0) == 0)
        def _():
            begin = 0
            for t in (first, *mids, total):
                step = t.shape[1]
                gb1[pl.ds(begin, step)] = (t[classes : classes + 1] * inv).reshape(step)
                gw2[:, begin : begin + step] = t[0:classes] * inv
                begin += step


def mix_grad_body(classes, n_states, *refs):
    scores, (first, logits, gamma, gmix, ggamma) = refs[:-5], refs[-5:]
    row = scores[0][0:1]
    for s in scores[1:]:
        row = row + s[0:1]
    row = row * (1.0 / pick(first[classes + 1 : classes + 2], classes + 1))
    weights = softmax_row(logits)
    mean = jnp.sum(weights * row, axis=1, keepdims=True)
    mix = gamma[0] * weights * (row - mean)
    lane = lax.broadcasted_iota(jnp.int32, mix.shape, 1)
    ggamma[0] = jnp.sum(mean)
    for s in range(n_states):
        gmix[s] = jnp.sum(jnp.where(lane == s, mix, 0.0))


def states_body(layers, classes, first, dmixed, logits, gamma, loss, gb2, grad):
    cols = grad.shape[2]
    section = lax.axis_index("section")
    half, tok = dmixed.shape[0], grad.shape[1]
    weights = softmax_row(logits)
    misc = first[classes + 1 : classes + 2]
    inv = 1.0 / pick(misc, classes + 1)

    @pl.when(pl.program_id(0) == 0)
    def _():
        loss[0] = jnp.sum(pick(misc, classes) * inv)
        for c in range(classes):
            gb2[c] = jnp.sum(pick(misc, c) * inv)

    d = dmixed[:, pl.ds(pl.multiple_of(pl.program_id(0) * cols, cols), cols)].astype(F32)
    row = lax.broadcasted_iota(jnp.int32, (16, d.shape[1]), 0)
    for l in range(layers):
        scaled = (gamma[0] * pick(weights, section * layers + l) * inv) * d
        grad[l, 0:16] = jnp.where(row == 0, 0.0, scaled[:16]).astype(BF16)
        grad[l, 16:half] = scaled[16:].astype(BF16)
        grad[l, half : half + 16] = jnp.where(row == 0, scaled[:1], 0.0).astype(BF16)
        grad[l, half + 16 :] = jnp.zeros((tok - half - 16, d.shape[1]), BF16)


def make_shards(n_section, n_dp):
    gather, reduce = split_dp(n_dp)
    n_gather, n_reduce = 1 << len(gather), 1 << len(reduce)

    def shards(states, mix_logits, mix_gamma, tag_w1, tag_b1, tag_w2, tag_b2, hyp_lengths, labels):
        layers, tok, width = states.shape
        ff = tag_w1.shape[1]
        classes = tag_b2.shape[0]
        n_states = mix_logits.shape[0]
        half = tok // 2
        rows = width // n_dp
        blocks = n_reduce // n_section
        share = blocks * rows
        widths = chunk_widths(ff)
        chunks = len(widths)
        extra = 2 * (-(-(classes + 3) // 8) * 8)
        cols = min(COLS, width)
        grid = (width // cols,)
        w2 = tag_w2.T
        states = pltpu.with_memory_space_constraint(states, pltpu.HBM)
        tag_w1 = pltpu.with_memory_space_constraint(tag_w1, pltpu.HBM)
        x_specs = [
            pl.BlockSpec((layers, half, cols), lambda i: (0, 0, i)),
            pl.BlockSpec((layers, 16, cols), lambda i: (0, half // 16, i)),
        ]
        col_spec = pl.BlockSpec((half, cols), lambda i: (0, i))

        wide = 256 if ff % 768 == 0 else 128
        third = ff // wide // 3
        cuts = [wide * n for n in (third, ff // wide - 2 * third, third)]
        w1_parts = [SDS((width, n), BF16) for n in cuts]
        term, wa = call(
            functools.partial(term_body, layers), grid, [SMEM] + x_specs + [ANY], (col_spec, VMEM),
            (SDS((half, width), BF16), w1_parts[0]), [pltpu.SemaphoreType.DMA],
        )(mix_logits, states, states, tag_w1)
        terms = [term] + others(term, "section", n_section)
        wb = call(
            functools.partial(load_body, cuts[0]), (1,), [ANY], VMEM, w1_parts[1], [pltpu.SemaphoreType.DMA],
        )(tag_w1)

        sends = (SDS((half, share), BF16),) * (n_gather - 1)
        mixed, *sends = call(
            functools.partial(mix_body, n_section, rows, blocks, gather, reduce), (1,),
            [VMEM] * n_section + [SMEM], (VMEM,) * n_gather, (SDS((half, width), BF16), *sends), limit=24,
        )(*terms, mix_gamma)
        gots = []
        for k, send in enumerate(sends, 1):
            got = flip(send, "dp", n_dp, spread(k, gather))
            gots += [got] + others(got, "section", n_section)

        hidden, slope, partial, wc = call(
            pre_body, (ff // wide,),
            [VMEM, VMEM, VMEM, ANY,
             pl.BlockSpec((1, wide), lambda i: (0, i)), pl.BlockSpec((classes, wide), lambda i: (0, i))],
            (pl.BlockSpec((half, wide), lambda i: (0, i)), pl.BlockSpec((half, wide), lambda i: (0, i)),
             whole((classes, half)), VMEM),
            (SDS((half, ff), BF16), SDS((half, ff), F32), SDS((classes, half), F32), w1_parts[2]),
            [pltpu.SemaphoreType.DMA],
        )(mixed, wa, wb, tag_w1, tag_b1.reshape(1, ff), w2)
        partials = [partial] + others(partial, "section", n_section)

        piece_shapes = [SDS((half + extra, step), BF16) for step in widths]
        dpre, *pieces = call(
            functools.partial(loss_body, n_section, widths, extra), (1,),
            [VMEM] * n_section + [SMEM, VMEM, SMEM, VMEM, VMEM, VMEM],
            (VMEM,) * (chunks + 1), (SDS((half, ff), BF16), *piece_shapes),
        )(*partials, tag_b2, labels.reshape(1, tok), hyp_lengths, w2, hidden, slope)

        tall = width // 8
        parts = []
        for h in range(2):
            part = call(
                functools.partial(dmixed_body, 4 * h), (4,), [VMEM] * 4,
                pl.BlockSpec((half, tall), lambda i: (0, i)), SDS((half, width // 2), BF16),
            )(dpre, wa, wb, wc)
            parts += [part] + others(part, "section", n_section)
        left = call(
            functools.partial(left_body, n_section, rows, blocks, reduce), (1,),
            [VMEM] * (1 + len(gots)), VMEM, SDS((n_reduce * rows, n_gather * half), BF16),
        )(mixed, *gots)
        cols = min(COLS, width // 2)
        grid = (width // cols,)
        x_specs[0] = pl.BlockSpec((layers, half, cols), lambda i: (0, 0, i))
        x_specs[1] = pl.BlockSpec((layers, 16, cols), lambda i: (0, half // 16, i))
        dmixed, score = call(
            functools.partial(score_body, n_section, layers), grid,
            [VMEM] * (2 * n_section) + x_specs, (VMEM, whole((8, 128))),
            (SDS((half, width), BF16), SDS((8, 128), F32)), limit=24,
        )(*parts, states, states)
        for group in (gather, reduce):
            scores = [score] + [flip(score, "dp", n_dp, spread(k, group)) for k in range(1, 1 << len(group))]
            score = call(total_body, (1,), [VMEM] * len(scores), VMEM, SDS((8, 128), F32))(*scores)
        scores = [score] + others(score, "section", n_section)

        strip = rows // 2
        totals, grad_w1 = [], None
        for c, step in enumerate(widths):
            begin = sum(widths[:c])
            total = SDS((extra // 2, step), F32)
            gathered = [pieces[c]] + [flip(pieces[c], "dp", n_dp, spread(k, gather)) for k in range(1, n_gather)]
            n = n_reduce // 2
            send, keep, small = call(
                functools.partial(weight_body, n_gather, half, reduce), (1,),
                [VMEM] * (1 + n_gather), (VMEM,) * 3,
                (SDS((n * rows + extra, step), BF16), SDS((n * rows, step), BF16), total),
                [pltpu.VMEM((n_gather * half, step), BF16), pltpu.VMEM((n_reduce * rows, step), BF16)],
            )(left, *gathered)
            for bit in reduce:
                got = flip(send, "dp", n_dp, bit)
                if n == 1:
                    break
                n //= 2
                send, keep, small = call(
                    functools.partial(add_body, rows), (1,), [VMEM] * 3, (VMEM,) * 3,
                    (SDS((n * rows + extra, step), BF16), SDS((n * rows, step), BF16), total),
                )(keep, got, small)
            args, specs = [keep, got, small], [VMEM] * 3
            outs = [SDS((rows, ff), F32), total]
            out_specs = [pl.BlockSpec((pl.Element(strip), pl.Element(step)), lambda i, b=begin: (i * strip, b)), whole(total.shape)]
            if c:
                args += [totals[0], grad_w1]
                specs += [VMEM, ANY]
            if c and c == chunks - 1:
                args += totals[1:]
                specs += [VMEM] * (chunks - 2)
                outs += [SDS((ff,), F32), SDS((classes, ff), F32)]
                out_specs += [VMEM, VMEM]
            grad_w1, tot, *others_out = call(
                functools.partial(final_body, c, chunks, classes), (rows // strip,),
                specs, tuple(out_specs), tuple(outs), aliases={4: 0} if c else {},
            )(*args)
            totals.append(tot)
            if c == 0:
                loss, grad_b2, grad_states = call(
                    functools.partial(states_body, layers, classes), grid,
                    [VMEM, VMEM, SMEM, SMEM],
                    (SMEM, SMEM, pl.BlockSpec((layers, tok, cols), lambda i: (0, 0, i))),
                    (SDS((1,), F32), SDS((classes,), F32), SDS((layers, tok, width), BF16)),
                )(tot, dmixed, mix_logits, mix_gamma)
        grad_mix, grad_gamma = call(
            functools.partial(mix_grad_body, classes, n_states), (1,),
            [VMEM] * (n_section + 1) + [SMEM, SMEM], (SMEM, SMEM), (SDS((n_states,), F32), SDS((1,), F32)),
        )(*scores, totals[0], mix_logits, mix_gamma)
        grad_b1, grad_w2 = others_out
        return (loss, grad_w1, grad_b1, grad_w2.T, grad_b2, grad_mix, grad_gamma, grad_states)

    return shards


def solution(mesh):
    in_specs = (
        P("section", "dp", None),
        P(),
        P(),
        P(None, "section"),
        P("section"),
        P("section", None),
        P(),
        P("dp"),
        P("dp"),
    )
    out_specs = (
        P(),
        P("dp", "section"),
        P("section"),
        P("section", None),
        P(),
        P(),
        P(),
        P("section", "dp", None),
    )
    shards = make_shards(mesh.shape["section"], mesh.shape["dp"])

    return jax.shard_map(shards, mesh=mesh, in_specs=in_specs, out_specs=out_specs, check_vma=False)
```

```python
import functools

import jax
import jax.numpy as jnp
from jax import lax
from jax.experimental import pallas as pl
from jax.experimental.pallas import tpu as pltpu
from jax.sharding import PartitionSpec as P


CHUNKS = 4
COLS = 2048
F32, BF16 = jnp.float32, jnp.bfloat16
SDS = jax.ShapeDtypeStruct
SMEM = pl.BlockSpec(memory_space=pltpu.SMEM)
VMEM = pl.BlockSpec(memory_space=pltpu.VMEM)
ANY = pl.BlockSpec(memory_space=pl.ANY)


def call(body, grid, in_specs, out_specs, out_shape, scratch=(), limit=12, aliases={}):
    return pl.pallas_call(
        body,
        grid_spec=pltpu.PrefetchScalarGridSpec(
            num_scalar_prefetch=0, grid=grid, in_specs=in_specs, out_specs=out_specs, scratch_shapes=list(scratch)
        ),
        out_shape=out_shape,
        input_output_aliases=aliases,
        compiler_params=pltpu.CompilerParams(vmem_limit_bytes=limit << 20),
    )


def whole(shape):
    return pl.BlockSpec(tuple(shape), lambda *_: (0,) * len(shape))


def flip(x, axis, size, bit):
    return lax.ppermute(x, axis, [(i, i ^ bit) for i in range(size)])


def others(x, axis, size):
    return [flip(x, axis, size, k) for k in range(1, size)]


def chunk_widths(ff):
    tiles = ff // 128
    count = min(CHUNKS, tiles)
    return [128 * ((tiles + c) // count) for c in range(count)]


def split_dp(n_dp):
    bits = [1 << b for b in range(n_dp.bit_length() - 1)]
    gather = bits[0::2][: len(bits) // 2]
    return gather, [b for b in bits if b not in gather]


def spread(r, bits):
    out = 0
    for i, bit in enumerate(bits):
        out = out | (((r >> i) & 1) * bit)
    return out


def compress(dp, bits):
    out = 0
    for i, bit in enumerate(bits):
        out = out | (((dp // bit) & 1) << i)
    return out


def softmax_row(logits):
    lane = lax.broadcasted_iota(jnp.int32, (1, 128), 1)
    row = jnp.full((1, 128), -jnp.inf, F32)
    for s in range(logits.shape[0]):
        row = jnp.where(lane == s, logits[s], row)
    expo = jnp.exp(row - jnp.max(row, axis=1, keepdims=True))
    return expo / jnp.sum(expo, axis=1, keepdims=True)


def pick(row, index):
    lane = lax.broadcasted_iota(jnp.int32, row.shape, 1)
    return jnp.sum(jnp.where(lane == index, row, 0.0), axis=1, keepdims=True)


def first_rows(x, last):
    row = lax.broadcasted_iota(jnp.int32, last.shape, 0)
    return jnp.where(row == 0, last[:1].astype(F32), x[:16].astype(F32))


def split16(x):
    high = x.astype(BF16)
    return jnp.concatenate([high.astype(F32), x - high.astype(F32)], 0).astype(BF16)


def join16(x):
    x = x.astype(F32)
    n = x.shape[0] // 2
    return x[:n] + x[n:]


def term_body(layers, logits, x, last, w1, out, w1_part, sem):
    step, load = pl.program_id(0), pltpu.make_async_copy(w1.at[:, pl.ds(0, w1_part.shape[1])], w1_part, sem)

    @pl.when(step == 0)
    def _():
        load.start()

    weights = softmax_row(logits)
    section = lax.axis_index("section")
    scale = [pick(weights, section * layers + l) for l in range(layers)]
    head = sum(scale[l] * first_rows(x[l], last[l]) for l in range(layers))
    rest = sum(scale[l] * x[l, 16:].astype(F32) for l in range(layers))
    out[:16] = head.astype(BF16)
    out[16:] = rest.astype(BF16)

    @pl.when(step == pl.num_programs(0) - 1)
    def _():
        load.wait()


def load_body(first, w1, w1_part, sem):
    load = pltpu.make_async_copy(w1.at[:, pl.ds(first, w1_part.shape[1])], w1_part, sem)
    load.start()
    load.wait()


def mix_body(n, rows, blocks, gather, reduce, *refs):
    terms, gamma, mixed, sends = refs[:n], refs[n], refs[n + 1], refs[n + 2 :]
    total = terms[0][...].astype(F32)
    for t in terms[1:]:
        total = total + t[...].astype(F32)
    mixed[...] = (gamma[0] * total).astype(BF16)
    section, dp = lax.axis_index("section"), lax.axis_index("dp")
    own = dp - spread(compress(dp, reduce), reduce)
    for k, send in enumerate(sends, 1):
        for i in range(blocks):
            at = (own ^ spread(k, gather)) + spread(section * blocks + i, reduce)
            send[:, i * rows : (i + 1) * rows] = mixed[:, pl.ds(pl.multiple_of(at * rows, rows), rows)]


def pre_body(mixed, wa, wb, w1, b1, w2, hidden, slope, logits, wc, sem):
    step, wide = pl.program_id(0), hidden.shape[1]
    begin = wa.shape[1] + wb.shape[1]
    load = pltpu.make_async_copy(w1.at[:, pl.ds(begin, wc.shape[1])], wc, sem)

    @pl.when(step == 0)
    def _():
        load.start()
        logits[...] = jnp.zeros_like(logits)

    @pl.when(step == begin // wide)
    def _():
        load.wait()

    def side(w, first):
        cols = w[:, pl.ds(pl.multiple_of((step - first) * wide, wide), wide)]
        pre = jnp.dot(mixed[...], cols, preferred_element_type=F32) + b1[...]
        cdf = 0.5 * (1.0 + lax.erf(pre * 0.7071067811865476))
        dens = jnp.exp(-0.5 * pre * pre) * 0.3989422804014327
        act = (pre * cdf).astype(BF16)
        hidden[...] = act
        slope[...] = cdf + pre * dens
        logits[...] += lax.dot_general(w2[...], act, (((1,), (1,)), ((), ())), preferred_element_type=F32)

    first = 0
    for w in (wa, wb, wc):
        count = w.shape[1] // wide
        pl.when((step >= first) & (step < first + count))(functools.partial(side, w, first))
        first += count


def loss_body(n, widths, extra, *refs):
    chunks = len(widths)
    parts = refs[:n]
    b2, labels, hyp, w2, hidden, slope = refs[n : n + 6]
    dpre, pieces = refs[n + 6], refs[n + 7 : n + 7 + chunks]
    logits = parts[0][...]
    for p in parts[1:]:
        logits = logits + p[...]
    classes, half = logits.shape
    kind = lax.broadcasted_iota(jnp.int32, logits.shape, 0)
    for c in range(classes):
        logits = logits + jnp.where(kind == c, b2[c], 0.0)
    lane = lax.broadcasted_iota(jnp.int32, (1, half), 1)
    mask = (jnp.where(lane == 0, half, lane) <= hyp[0]).astype(F32)
    lab = labels[...]
    lab = jnp.where(lane == 0, lab[:, half : half + 1], lab[:, :half])
    onehot = (kind == lab).astype(F32)
    expl = jnp.exp(logits)
    totals = jnp.sum(expl, axis=0, keepdims=True)
    entropy = jnp.log(totals) - jnp.sum(logits * onehot, axis=0, keepdims=True)
    dlogits = mask * (expl / totals - onehot)
    dlog16 = dlogits.astype(BF16)
    dhidden = lax.dot_general(dlog16, w2[...], (((0,), (0,)), ((), ())), preferred_element_type=F32)
    grad = (dhidden * slope[...]).astype(BF16)
    dpre[...] = grad
    ff = grad.shape[1]
    grad_w2 = lax.dot_general(dlog16, hidden[...], (((1,), (0,)), ((), ())), preferred_element_type=F32)
    grad_b1 = jnp.sum(grad.astype(F32), axis=0, keepdims=True)
    col = lax.broadcasted_iota(jnp.int32, (1, ff), 1)
    row = jnp.where(col == classes, jnp.sum(mask * entropy), 0.0)
    row = jnp.where(col == classes + 1, jnp.sum(mask), row)
    sums = jnp.sum(dlogits, axis=1, keepdims=True)
    for c in range(classes):
        row = jnp.where(col == c, sums[c : c + 1], row)
    rows = [grad_w2, grad_b1, row]
    if extra // 2 > classes + 2:
        rows.append(jnp.zeros((extra // 2 - classes - 2, ff), F32))
    small = split16(jnp.concatenate(rows, 0))
    start = 0
    for piece, step in zip(pieces, widths):
        piece[0:half] = grad[:, start : start + step]
        piece[half:] = small[:, start : start + step]
        start += step


def dmixed_body(base, dpre, wa, wb, wc, out):
    tall = out.shape[1]
    row = pl.multiple_of((pl.program_id(0) + base) * tall, tall)
    total, col = None, 0
    for w in (wa, wb, wc):
        n = w.shape[1]
        part = lax.dot_general(
            dpre[:, col : col + n], w[pl.ds(row, tall)], (((1,), (1,)), ((), ())), preferred_element_type=F32
        )
        total = part if total is None else total + part
        col += n
    out[...] = total.astype(BF16)


def score_body(n, layers, *refs):
    parts, x, last, dmixed, scores = refs[: 2 * n], refs[2 * n], refs[2 * n + 1], refs[2 * n + 2], refs[2 * n + 3]
    step, steps = pl.program_id(0), pl.num_programs(0)

    @pl.when(step == 0)
    def _():
        scores[...] = jnp.zeros_like(scores)

    cols = x.shape[2]

    def side(some, first):
        at = pl.ds(pl.multiple_of((step - first) * cols, cols), cols)
        total = some[0][:, at].astype(F32)
        for p in some[1:]:
            total = total + p[:, at].astype(F32)
        d16 = total.astype(BF16)
        dmixed[:, pl.ds(pl.multiple_of(step * cols, cols), cols)] = d16
        d = d16.astype(F32)
        lane = lax.broadcasted_iota(jnp.int32, (1, 128), 1)
        section = lax.axis_index("section")
        for l in range(layers):
            prod = jnp.sum(first_rows(x[l], last[l]) * d[:16], axis=0, keepdims=True)
            prod = prod + jnp.sum(x[l, 16:].astype(F32) * d[16:], axis=0, keepdims=True)
            score = jnp.sum(prod, axis=1, keepdims=True)
            scores[0:1] += jnp.where(lane == section * layers + l, score, 0.0)

    @pl.when(step < steps // 2)
    def _():
        side(parts[:n], 0)

    @pl.when(step >= steps // 2)
    def _():
        side(parts[n:], steps // 2)


def total_body(*refs):
    total = refs[0][...]
    for s in refs[1:-1]:
        total = total + s[...]
    refs[-1][...] = total


def left_body(n, rows, blocks, reduce, *refs):
    mixed, gots, out = refs[0], refs[1:-1], refs[-1]
    section, dp = lax.axis_index("section"), lax.axis_index("dp")
    own = dp - spread(compress(dp, reduce), reduce)
    share = rows * blocks
    for j in range(n):
        cols = []
        for i in range(blocks):
            at = own + spread((section ^ j) * blocks + i, reduce)
            cols.append(mixed[:, pl.ds(pl.multiple_of(at * rows, rows), rows)])
        parts = [jnp.concatenate(cols, 1)] + [got[...] for got in gots[j::n]]
        out[pl.ds(pl.multiple_of((section ^ j) * share, share), share)] = jnp.concatenate(parts, 0).T


def halves(blocks, tail, send, keep, block_of, rows):
    for out, parity in ((send, 1), (keep, 0)):
        for i in range(blocks // 2):
            out[i * rows : (i + 1) * rows] = block_of(2 * i + parity)
    send[blocks // 2 * rows :] = tail


def weight_body(n_gather, half, reduce, *refs):
    left, pieces, (send, keep, small, rhs, prod) = refs[0], refs[1 : 1 + n_gather], refs[1 + n_gather :]
    r = compress(lax.axis_index("dp"), reduce)
    total = None
    for k, piece in enumerate(pieces):
        rhs[k * half : (k + 1) * half] = piece[:half]
        own = join16(piece[half:])
        total = own if total is None else total + own
    prod[...] = jnp.dot(left[...], rhs[...], preferred_element_type=F32).astype(BF16)
    small[...] = total
    blocks = 1 << len(reduce)
    rows = prod.shape[0] // blocks
    halves(
        blocks, split16(total), send, keep,
        lambda j: prod[pl.ds(pl.multiple_of((r ^ j) * rows, rows), rows)], rows,
    )


def add_body(rows, kept, got, small_in, send, keep, small):
    base = kept.shape[0]
    total = small_in[...] + join16(got[base:])
    small[...] = total
    block = lambda j: (
        kept[j * rows : (j + 1) * rows].astype(F32) + got[j * rows : (j + 1) * rows].astype(F32)
    ).astype(BF16)
    halves(base // rows, split16(total), send, keep, block, rows)


def final_body(chunk, chunks, classes, kept, got, small, *refs):
    if chunk:
        first, refs = refs[0], refs[2:]
    last = chunk == chunks - 1 and chunk > 0
    if last:
        mids, refs = refs[: chunks - 2], refs[chunks - 2 :]
    grad, total = refs[0], refs[1]
    strip = grad.shape[0]

    @pl.when(pl.program_id(0) == 0)
    def _():
        total[...] = small[...] + join16(got[kept.shape[0] :])

    misc = (first if chunk else total)[classes + 1 : classes + 2]
    inv = 1.0 / pick(misc, classes + 1)
    start = pl.multiple_of(pl.program_id(0) * strip, strip)
    grad[...] = (kept[pl.ds(start, strip)].astype(F32) + got[pl.ds(start, strip)].astype(F32)) * inv
    if last:
        gb1, gw2 = refs[2:]

        @pl.when(pl.program_id(0) == 0)
        def _():
            begin = 0
            for t in (first, *mids, total):
                step = t.shape[1]
                gb1[pl.ds(begin, step)] = (t[classes : classes + 1] * inv).reshape(step)
                gw2[:, begin : begin + step] = t[0:classes] * inv
                begin += step


def mix_grad_body(classes, n_states, *refs):
    scores, (first, logits, gamma, gmix, ggamma) = refs[:-5], refs[-5:]
    row = scores[0][0:1]
    for s in scores[1:]:
        row = row + s[0:1]
    row = row * (1.0 / pick(first[classes + 1 : classes + 2], classes + 1))
    weights = softmax_row(logits)
    mean = jnp.sum(weights * row, axis=1, keepdims=True)
    mix = gamma[0] * weights * (row - mean)
    lane = lax.broadcasted_iota(jnp.int32, mix.shape, 1)
    ggamma[0] = jnp.sum(mean)
    for s in range(n_states):
        gmix[s] = jnp.sum(jnp.where(lane == s, mix, 0.0))


def states_body(layers, classes, first, dmixed, logits, gamma, loss, gb2, grad):
    cols = grad.shape[2]
    section = lax.axis_index("section")
    half, tok = dmixed.shape[0], grad.shape[1]
    weights = softmax_row(logits)
    misc = first[classes + 1 : classes + 2]
    inv = 1.0 / pick(misc, classes + 1)

    @pl.when(pl.program_id(0) == 0)
    def _():
        loss[0] = jnp.sum(pick(misc, classes) * inv)
        for c in range(classes):
            gb2[c] = jnp.sum(pick(misc, c) * inv)

    d = dmixed[:, pl.ds(pl.multiple_of(pl.program_id(0) * cols, cols), cols)].astype(F32)
    row = lax.broadcasted_iota(jnp.int32, (16, d.shape[1]), 0)
    for l in range(layers):
        scaled = (gamma[0] * pick(weights, section * layers + l) * inv) * d
        grad[l, 0:16] = jnp.where(row == 0, 0.0, scaled[:16]).astype(BF16)
        grad[l, 16:half] = scaled[16:].astype(BF16)
        grad[l, half : half + 16] = jnp.where(row == 0, scaled[:1], 0.0).astype(BF16)
        grad[l, half + 16 :] = jnp.zeros((tok - half - 16, d.shape[1]), BF16)


def make_shards(n_section, n_dp):
    gather, reduce = split_dp(n_dp)
    n_gather, n_reduce = 1 << len(gather), 1 << len(reduce)

    def shards(states, mix_logits, mix_gamma, tag_w1, tag_b1, tag_w2, tag_b2, hyp_lengths, labels):
        layers, tok, width = states.shape
        ff = tag_w1.shape[1]
        classes = tag_b2.shape[0]
        n_states = mix_logits.shape[0]
        half = tok // 2
        rows = width // n_dp
        blocks = n_reduce // n_section
        share = blocks * rows
        widths = chunk_widths(ff)
        chunks = len(widths)
        extra = 2 * (-(-(classes + 3) // 8) * 8)
        cols = min(2048, width)
        grid = (width // cols,)
        w2 = tag_w2.T
        states = pltpu.with_memory_space_constraint(states, pltpu.HBM)
        mix_logits = pltpu.with_memory_space_constraint(mix_logits, pltpu.HBM)
        tag_w1 = pltpu.with_memory_space_constraint(tag_w1, pltpu.HBM)
        x_specs = [
            pl.BlockSpec((layers, half, cols), lambda i: (0, 0, i)),
            pl.BlockSpec((layers, 16, cols), lambda i: (0, half // 16, i)),
        ]
        col_spec = pl.BlockSpec((half, cols), lambda i: (0, i))

        wide = 256 if ff % 768 == 0 else 128
        part = ff // wide // 6
        cuts = [wide * n for n in (1 * part, 2 * part, ff // wide - 3 * part)] if part else [wide] * 3
        w1_parts = [SDS((width, n), BF16) for n in cuts]
        term, wa = call(
            functools.partial(term_body, layers), grid, [SMEM] + x_specs + [ANY], (col_spec, VMEM),
            (SDS((half, width), BF16), w1_parts[0]), [pltpu.SemaphoreType.DMA],
        )(mix_logits, states, states, tag_w1)
        terms = [term] + others(term, "section", n_section)
        wb = call(
            functools.partial(load_body, cuts[0]), (1,), [ANY], VMEM, w1_parts[1], [pltpu.SemaphoreType.DMA],
        )(tag_w1)

        sends = (SDS((half, share), BF16),) * (n_gather - 1)
        mixed, *sends = call(
            functools.partial(mix_body, n_section, rows, blocks, gather, reduce), (1,),
            [VMEM] * n_section + [SMEM], (VMEM,) * n_gather, (SDS((half, width), BF16), *sends), limit=24,
        )(*terms, mix_gamma)
        gots = []
        for k, send in enumerate(sends, 1):
            got = flip(send, "dp", n_dp, spread(k, gather))
            gots += [got] + others(got, "section", n_section)

        hidden, slope, partial, wc = call(
            pre_body, (ff // wide,),
            [VMEM, VMEM, VMEM, ANY,
             pl.BlockSpec((1, wide), lambda i: (0, i)), pl.BlockSpec((classes, wide), lambda i: (0, i))],
            (pl.BlockSpec((half, wide), lambda i: (0, i)), pl.BlockSpec((half, wide), lambda i: (0, i)),
             whole((classes, half)), VMEM),
            (SDS((half, ff), BF16), SDS((half, ff), F32), SDS((classes, half), F32), w1_parts[2]),
            [pltpu.SemaphoreType.DMA],
        )(mixed, wa, wb, tag_w1, tag_b1.reshape(1, ff), w2)
        partials = [partial] + others(partial, "section", n_section)

        piece_shapes = [SDS((half + extra, step), BF16) for step in widths]
        dpre, *pieces = call(
            functools.partial(loss_body, n_section, widths, extra), (1,),
            [VMEM] * n_section + [SMEM, VMEM, SMEM, VMEM, VMEM, VMEM],
            (VMEM,) * (chunks + 1), (SDS((half, ff), BF16), *piece_shapes),
        )(*partials, tag_b2, labels.reshape(1, tok), hyp_lengths, w2, hidden, slope)

        tall = width // 8
        parts = []
        for h in range(2):
            part = call(
                functools.partial(dmixed_body, 4 * h), (4,), [VMEM] * 4,
                pl.BlockSpec((half, tall), lambda i: (0, i)), SDS((half, width // 2), BF16),
            )(dpre, wa, wb, wc)
            parts += [part] + others(part, "section", n_section)
        left = call(
            functools.partial(left_body, n_section, rows, blocks, reduce), (1,),
            [VMEM] * (1 + len(gots)), VMEM, SDS((n_reduce * rows, n_gather * half), BF16),
        )(mixed, *gots)
        cols = min(COLS, width // 2)
        grid = (width // cols,)
        x_specs[0] = pl.BlockSpec((layers, half, cols), lambda i: (0, 0, i))
        x_specs[1] = pl.BlockSpec((layers, 16, cols), lambda i: (0, half // 16, i))
        dmixed, score = call(
            functools.partial(score_body, n_section, layers), grid,
            [VMEM] * (2 * n_section) + x_specs, (VMEM, whole((8, 128))),
            (SDS((half, width), BF16), SDS((8, 128), F32)), limit=24,
        )(*parts, states, states)
        for group in (gather, reduce):
            scores = [score]
            for k in range(1, 1 << len(group)):
                scores.append(flip(score, "dp", n_dp, spread(k, group)))
            score = call(total_body, (1,), [VMEM] * len(scores), VMEM, SDS((8, 128), F32))(*scores)
        scores = [score] + others(score, "section", n_section)

        strip = rows // 2
        totals, grad_w1 = [], None
        for c, step in enumerate(widths):
            begin = sum(widths[:c])
            total = SDS((extra // 2, step), F32)
            gathered = [pieces[c]]
            for k in range(1, n_gather):
                gathered.append(flip(pieces[c], "dp", n_dp, spread(k, gather)))
            n = n_reduce // 2
            send, keep, small = call(
                functools.partial(weight_body, n_gather, half, reduce), (1,),
                [VMEM] * (1 + n_gather), (VMEM,) * 3,
                (SDS((n * rows + extra, step), BF16), SDS((n * rows, step), BF16), total),
                [pltpu.VMEM((n_gather * half, step), BF16), pltpu.VMEM((n_reduce * rows, step), BF16)],
            )(left, *gathered)
            for bit in reduce:
                got = flip(send, "dp", n_dp, bit)
                if n == 1:
                    break
                n //= 2
                send, keep, small = call(
                    functools.partial(add_body, rows), (1,), [VMEM] * 3, (VMEM,) * 3,
                    (SDS((n * rows + extra, step), BF16), SDS((n * rows, step), BF16), total),
                )(keep, got, small)
            args, specs = [keep, got, small], [VMEM] * 3
            outs = [SDS((rows, ff), F32), total]
            out_specs = [pl.BlockSpec((pl.Element(strip), pl.Element(step)), lambda i, b=begin: (i * strip, b)), whole(total.shape)]
            if c:
                args += [totals[0], grad_w1]
                specs += [VMEM, ANY]
            if c and c == chunks - 1:
                args += totals[1:]
                specs += [VMEM] * (chunks - 2)
                outs += [SDS((ff,), F32), SDS((classes, ff), F32)]
                out_specs += [VMEM, VMEM]
            grad_w1, tot, *others_out = call(
                functools.partial(final_body, c, chunks, classes), (rows // strip,),
                specs, tuple(out_specs), tuple(outs), aliases={4: 0} if c else {},
            )(*args)
            totals.append(tot)
            if c == 0:
                loss, grad_b2, grad_states = call(
                    functools.partial(states_body, layers, classes), grid,
                    [VMEM, VMEM, SMEM, SMEM],
                    (SMEM, SMEM, pl.BlockSpec((layers, tok, cols), lambda i: (0, 0, i))),
                    (SDS((1,), F32), SDS((classes,), F32), SDS((layers, tok, width), BF16)),
                )(tot, dmixed, mix_logits, mix_gamma)
        grad_mix, grad_gamma = call(
            functools.partial(mix_grad_body, classes, n_states), (1,),
            [VMEM] * (n_section + 1) + [SMEM, SMEM], (SMEM, SMEM), (SDS((n_states,), F32), SDS((1,), F32)),
        )(*scores, totals[0], mix_logits, mix_gamma)
        grad_b1, grad_w2 = others_out
        return (loss, grad_w1, grad_b1, grad_w2.T, grad_b2, grad_mix, grad_gamma, grad_states)

    return shards


def solution(mesh):
    in_specs = (
        P("section", "dp", None),
        P(),
        P(),
        P(None, "section"),
        P("section"),
        P("section", None),
        P(),
        P("dp"),
        P("dp"),
    )
    out_specs = (
        P(),
        P("dp", "section"),
        P("section"),
        P("section", None),
        P(),
        P(),
        P(),
        P("section", "dp", None),
    )
    shards = make_shards(mesh.shape["section"], mesh.shape["dp"])

    return jax.shard_map(shards, mesh=mesh, in_specs=in_specs, out_specs=out_specs, check_vma=False)
```
